32 devices in a mesh: grp: 8 (over z, core), row: 4 (over y, x).
Axes of the slice: x: 2, y: 2, z: 4, core: 2. Of those that a mesh axis runs over, the one named last changes fastest.
Arguments:
- theta: float32 [16, 512, 512], P('grp', 'row'), may hold values from -8 to 8
- left_env: bfloat16 [16, 8, 512, 512], P('grp', None, 'row'), may hold values from -1.5 to 1.5
- right_env: bfloat16 [16, 8, 512, 512], P('grp', None, 'row'), may hold values from -3.5 to 3.5
- lengths: int32 [16, 2], P('grp'), may hold values from 128 to 512
Outputs:
- evolved: float32 [16, 512, 512], P('grp', 'row')
- hessenberg: float32 [8, 8], replicated
The draws below stay inside these ranges and needn't reach their ends.
All inputs are finite; a program needn't handle non-finite values.
Results may differ from the reference program's by a relative error of at most 0.0029.
Values may be sent and summed in bfloat16 or wider, within the bound.
A program may use at most 64 MiB of HBM per device.

```python
import jax
import jax.numpy as jnp
from jax import lax

SECT = 512
TERMS = 8
KRYLOV = 8
SECTORS = 16


def draw_theta(key, part):
    sector_pos = jnp.arange(SECTORS, dtype=jnp.float32) / max(SECTORS - 1, 1)
    base = jnp.clip(jax.random.normal(key, (SECTORS, SECT, SECT), jnp.float32), -3.2, 3.2)
    scales = 0.4 * 6.0 ** sector_pos
    return (base * scales[:, None, None]).astype(jnp.float32)


def draw_left_env(key, part):
    noise_key = jax.random.fold_in(key, 11)
    noise = jnp.clip(jax.random.normal(noise_key, (SECTORS, TERMS, SECT, SECT), jnp.float32), -4.0, 4.0)
    noise = noise * (SECT * TERMS) ** (-0.5)
    identity = jnp.eye(SECT, dtype=jnp.float32)
    first = (jnp.arange(TERMS) == 0).astype(jnp.float32)
    return (noise + first[None, :, None, None] * identity[None, None, :, :]).astype(jnp.bfloat16)


def draw_right_env(key, part):
    noise_key = jax.random.fold_in(key, 23)
    rate_key = jax.random.fold_in(key, 37)
    noise = jnp.clip(jax.random.normal(noise_key, (SECTORS, TERMS, SECT, SECT), jnp.float32), -4.0, 4.0)
    rates = jax.random.uniform(rate_key, (SECTORS,), jnp.float32, 0.5, 2.0)
    noise = noise * SECT ** (-0.5)
    identity = jnp.eye(SECT, dtype=jnp.float32)
    first = (jnp.arange(TERMS) == 0).astype(jnp.float32)
    return (noise - (rates[:, None] * first[None, :])[:, :, None, None] * identity[None, None, :, :]).astype(jnp.bfloat16)


def plant(result, key, least, top_value):
    dims = result.shape
    place = [jax.random.randint(jax.random.fold_in(key, axis), (), 0, dims[axis]) for axis in range(len(dims))]
    result = result.at[tuple(place)].set(least)
    longest = dims.index(max(dims))
    place[longest] = (place[longest] + 1) % dims[longest]
    return result.at[tuple(place)].set(top_value)


def setup_inputs(seed: int = 0) -> dict:
    key_list = jax.random.split(jax.random.key(seed), 5)
    return {
        "theta": draw_theta(jax.random.fold_in(key_list[4], 71), 0),
        "left_env": draw_left_env(jax.random.fold_in(key_list[4], 71), 0),
        "right_env": draw_right_env(jax.random.fold_in(key_list[4], 71), 0),
        "lengths": plant(jax.random.randint(key_list[3], (SECTORS, 2), SECT // 4, SECT + 1), jax.random.fold_in(key_list[3], 1), SECT // 4, SECT).astype(jnp.int32),
    }


epsilon = 1e-06
time_step = 0.5

def live_of(lengths):
    row_ids = lax.broadcasted_iota(jnp.int32, (1, SECT, 1), 1)
    col_ids = lax.broadcasted_iota(jnp.int32, (1, 1, SECT), 2)
    return ((row_ids < lengths[:, 0][:, None, None]) & (col_ids < lengths[:, 1][:, None, None])).astype(jnp.float32)

def apply_sector(operands):
    vector, left_one, right_one = operands
    packed = lax.optimization_barrier(vector.astype(jnp.bfloat16)).astype(jnp.float32)
    inner_terms = jnp.einsum('ab,wbc->wac', packed, right_one.astype(jnp.float32), precision=lax.Precision.HIGHEST)
    inner_terms = lax.optimization_barrier(inner_terms.astype(jnp.bfloat16)).astype(jnp.float32)
    return jnp.einsum('wba,wbc->ac', left_one.astype(jnp.float32), inner_terms, precision=lax.Precision.HIGHEST)

def propagate(hessenberg):
    scaled = time_step * hessenberg
    series = jnp.eye(KRYLOV, dtype=jnp.float32)
    series_term = jnp.eye(KRYLOV, dtype=jnp.float32)
    for degree in range(1, 19):
        series_term = jnp.dot(series_term, scaled, precision=lax.Precision.HIGHEST) / degree
        series = series + series_term
    return series[:, 0]

def reference(theta, left_env, right_env, lengths):
    live_mask = live_of(lengths)
    start_block = theta * live_mask
    norm_zero = jnp.sqrt(jnp.sum(start_block * start_block) + epsilon)
    krylov_basis = [start_block / norm_zero]
    hessenberg = jnp.zeros((KRYLOV, KRYLOV), jnp.float32)
    for column in range(KRYLOV):
        image = lax.map(apply_sector, (krylov_basis[column], left_env, right_env)) * live_mask
        coefficients = jnp.stack([jnp.sum(vector * image) for vector in krylov_basis])
        for previous in range(column + 1):
            image = image - coefficients[previous] * krylov_basis[previous]
        hessenberg = hessenberg.at[:column + 1, column].set(coefficients)
        if column + 1 < KRYLOV:
            beta_norm = jnp.sqrt(jnp.sum(image * image) + epsilon)
            hessenberg = hessenberg.at[column + 1, column].set(beta_norm)
            krylov_basis.append(image / beta_norm)
    weights = propagate(hessenberg)
    evolved = jnp.zeros_like(start_block)
    for column in range(KRYLOV):
        evolved = evolved + weights[column] * krylov_basis[column]
    return (norm_zero * evolved, hessenberg)
```

```python
import functools

import jax
import jax.numpy as jnp
from jax import lax
from jax.experimental import pallas as pl
from jax.experimental.pallas import tpu as pltpu
from jax.sharding import PartitionSpec as P

KRYLOV = 8
DEGREES = 19
ROWS = 64

epsilon = 1e-06
time_step = 0.5
MESH = pl.DeviceIdType.MESH
F32 = jnp.float32
BF16 = jnp.bfloat16


def kernel(ngrp, nrow, lengths, theta, left, right, out, hess,
           masked, meta, l_land, l_t, r_land, q, basis, v, acc, live, msg, slots, h_t, evolved,
           th_send, th_recv, meta_send, meta_recv, l_send, l_recv, f_send, f_recv,
           r_send, r_recv, v_send, v_recv, m_send, m_recv, o_send, o_recv):
    S, lr, width = theta.shape
    W = left.shape[1]
    half = width // 2
    K = KRYLOV
    n = ngrp * nrow
    rep = nrow // (2 * S)
    g, r = lax.axis_index("grp"), lax.axis_index("row")
    me = g * nrow + r
    p = g % 2
    base = g - p
    partner = (base + 1 - p, r)
    owner = r // (S * rep)
    sector = (r // rep) % S
    my_cols = pl.ds(pl.multiple_of(p * half, half), half)
    my_rows = pl.ds(pl.multiple_of(r * lr, lr), lr)

    barrier = pltpu.get_barrier_semaphore()

    def greet(o, c):
        t = (me + o) % n
        pl.semaphore_signal(barrier, inc=1, device_id=(t // nrow, t % nrow), device_id_type=MESH)
        return c

    lax.fori_loop(1, n, greet, 0)

    lane = lax.broadcasted_iota(jnp.int32, (1, 128), 1)
    square = jnp.zeros((8, width), F32)
    for s in range(S):
        for k in range(2):
            meta[p, pl.ds(2 * s + k, 1), :] = jnp.full((1, 128), lengths[s, k].astype(F32))
        row_ids = r * lr + lax.broadcasted_iota(jnp.int32, (lr, width), 0)
        col_ids = lax.broadcasted_iota(jnp.int32, (lr, width), 1)
        keep = (row_ids < lengths[s, 0]) & (col_ids < lengths[s, 1])
        block = jnp.where(keep, theta[s], 0.0)
        masked[s] = block
        square = square + jnp.sum((block * block).reshape(lr // 8, 8, width), axis=0)
    for k in range(1, K):
        basis[k] = jnp.zeros((width, half), F32)
    h_t[...] = jnp.zeros_like(h_t)

    pl.semaphore_wait(barrier, n - 1)

    def put(src, dst, send, recv, dev, own):
        @pl.when(own)
        def _():
            pltpu.make_async_copy(src, dst, recv).start()

        @pl.when(jnp.logical_not(own))
        def _():
            pltpu.make_async_remote_copy(src_ref=src, dst_ref=dst, send_sem=send, recv_sem=recv,
                                         device_id=dev, device_id_type=MESH).start()

    def put_done(src, send, own):
        @pl.when(jnp.logical_not(own))
        def _():
            pltpu.make_async_copy(src, src, send).wait()

    def got(dst, recv):
        pltpu.make_async_copy(dst, dst, recv).wait()

    def share(k, row):
        msg[k] = row
        slots[k, me] = row

        def one(o, c):
            t = (me + o) % n
            pltpu.make_async_remote_copy(src_ref=msg.at[k], dst_ref=slots.at[k, me], send_sem=m_send.at[k],
                                         recv_sem=m_recv.at[k], device_id=(t // nrow, t % nrow),
                                         device_id_type=MESH).start()
            return c

        lax.fori_loop(1, n, one, 0)

    def shared(k):
        rest = slots.at[k, pl.ds(0, n - 1)]
        pltpu.make_async_copy(rest, rest, m_recv.at[k]).wait()
        pltpu.make_async_copy(rest, rest, m_send.at[k]).wait()
        return jnp.sum(slots[k], axis=0)

    def pick(row, i):
        return jnp.sum(jnp.where(lane == i, row, 0.0), axis=1, keepdims=True)

    meta_copy = pltpu.make_async_remote_copy(src_ref=meta.at[p], dst_ref=meta.at[p], send_sem=meta_send,
                                             recv_sem=meta_recv, device_id=partner, device_id_type=MESH)
    meta_copy.start()
    share(K, jnp.where(lane == 0, jnp.sum(square), 0.0))

    targets = [(s, j, (p * S + s) * rep + j) for s in range(S) for j in range(rep)]

    def theta_piece(s, c):
        return masked.at[s, :, pl.ds(c * half, half)]

    for s, j, t in targets:
        for c in range(2):
            put(theta_piece(s, c), basis.at[0, my_rows, :], th_send.at[s, j, c], th_recv.at[r],
                (base + c, t), (t == r) & (p == c))

    def env(w, carry):
        for s, j, t in targets:
            for c in range(2):
                put(right.at[s, w, :, pl.ds(c * half, half)], r_land.at[w, my_rows, :],
                    r_send.at[w, s, j, c], r_recv.at[w, r], (base + c, t), (t == r) & (p == c))
            put(left.at[s, w], l_land.at[w, my_rows, :], l_send.at[w, s, j], l_recv.at[w, r],
                (base + w % 2, t), (t == r) & (p == w % 2))
        return carry

    lax.fori_loop(0, W, env, 0)

    pltpu.make_async_copy(meta.at[1 - p], meta.at[1 - p], meta_recv).wait()
    a_len = meta[owner, pl.ds(2 * sector, 1), :]
    c_len = meta[owner, pl.ds(2 * sector + 1, 1), :]
    a_len = jnp.concatenate([a_len] * (half // 128), axis=1)
    c_len = jnp.concatenate([c_len] * (half // 128), axis=1)
    row_ids = lax.broadcasted_iota(jnp.int32, (width, half), 0).astype(F32)
    col_ids = (p * half + lax.broadcasted_iota(jnp.int32, (width, half), 1)).astype(F32)
    live[...] = jnp.where((row_ids < a_len) & (col_ids < c_len), 1.0, 0.0)

    def v_copy(j):
        return pltpu.make_async_remote_copy(src_ref=v.at[j, :, my_cols], dst_ref=v.at[j, :, my_cols],
                                            send_sem=v_send.at[j], recv_sem=v_recv.at[j],
                                            device_id=partner, device_id_type=MESH)

    norm_zero = jnp.sqrt(pick(shared(K), 0) + epsilon)
    for i in range(nrow):
        got(basis.at[0, pl.ds(i * lr, lr), :], th_recv.at[i])

    def start_chunk(i, c):
        rows = pl.ds(pl.multiple_of(i * ROWS, ROWS), ROWS)
        b = basis[0, rows, :] / norm_zero
        basis[0, rows, :] = b
        v[0, rows, my_cols] = b.astype(BF16)
        return c

    lax.fori_loop(0, width // ROWS, start_chunk, 0)
    first = v_copy(0)
    first.start()
    first.wait()

    def forward_copy(w):
        return pltpu.make_async_remote_copy(src_ref=l_land.at[w], dst_ref=l_land.at[w], send_sem=f_send.at[w],
                                            recv_sem=f_recv.at[w], device_id=partner, device_id_type=MESH)

    def image_zero(pair, carry):
        mine = 2 * pair + p
        for i in range(nrow):
            got(l_land.at[mine, pl.ds(i * lr, lr), :], l_recv.at[mine, i])
        forward_copy(mine).start()
        for step in range(2):
            w = 2 * pair + step
            for i in range(nrow):
                got(r_land.at[w, pl.ds(i * lr, lr), :], r_recv.at[w, i])
            at = pl.ds(pl.multiple_of(w * width, width), width)
            q[at, :] = jnp.dot(v[0], r_land[w], preferred_element_type=F32).astype(BF16)
        theirs = 2 * pair + 1 - p
        got(l_land.at[theirs], f_recv.at[theirs])
        for step in range(2):
            w = 2 * pair + step
            at = pl.ds(pl.multiple_of(w * width, width), width)
            l_t[:, at] = l_land[w].T
        return carry

    lax.fori_loop(0, W // 2, image_zero, 0)

    def outer():
        acc[...] = jnp.dot(l_t[...], q[...], preferred_element_type=F32)

    outer()

    counts = jnp.where(r % rep == 0, 1.0, 0.0)

    def coefficients(j):
        def chunk(i, sums):
            rows = pl.ds(pl.multiple_of(i * ROWS, ROWS), ROWS)
            u = acc[rows, :] * live[rows, :]
            acc[rows, :] = u
            new = []
            for k in range(K + 1):
                other = basis[k, rows, :] if k < K else u
                new.append(sums[k] + jnp.sum((other * u).reshape(ROWS // 8, 8, half), axis=0))
            return tuple(new)

        zero = jnp.zeros((8, half), F32)
        sums = lax.fori_loop(0, width // ROWS, chunk, (zero,) * (K + 1))
        row = jnp.zeros((1, 128), F32)
        for k in range(K + 1):
            row = jnp.where(lane == k, jnp.sum(sums[k]), row)
        share(j, row * counts)
        return shared(j)

    def step(j, carry):
        row = coefficients(j)
        dots = jnp.where(lane < K, row, 0.0)
        left_over = pick(row, K) - jnp.sum(dots * dots, axis=1, keepdims=True)
        beta = jnp.sqrt(jnp.maximum(left_over, 0.0) + epsilon)
        h_t[pl.ds(j, 1), :] = jnp.where(lane == j + 1, beta, dots)
        coef = [pick(row, k) for k in range(K)]
        scale = 1.0 / beta

        def chunk(i, c):
            rows = pl.ds(pl.multiple_of(i * ROWS, ROWS), ROWS)
            u = acc[rows, :]
            for k in range(K):
                u = u - coef[k] * basis[k, rows, :]
            u = u * scale
            basis[j + 1, rows, :] = u
            v[j + 1, rows, my_cols] = u.astype(BF16)
            return c

        lax.fori_loop(0, width // ROWS, chunk, 0)
        copy = v_copy(j + 1)
        copy.start()
        copy.wait()
        vec = v.at[j + 1]

        for w in range(W):
            q[w * width:(w + 1) * width, :] = jnp.dot(vec[...], r_land[w], preferred_element_type=F32).astype(BF16)
        outer()
        return carry

    lax.fori_loop(0, K - 1, step, 0)
    row = coefficients(K - 1)
    h_t[pl.ds(K - 1, 1), :] = jnp.where(lane < K, row, 0.0)

    ht = h_t[...]
    sub = lax.broadcasted_iota(jnp.int32, (K, 128), 0)
    lanes = lax.broadcasted_iota(jnp.int32, (K, 128), 1)
    h = jnp.zeros((K, 128), F32)
    for j in range(K):
        column = jnp.sum(jnp.where(lanes == sub, ht[j:j + 1, :], 0.0), axis=1, keepdims=True)
        h = jnp.where(lanes == j, column, h)
    hess[...] = h[:, :K]
    term = jnp.where(lane == 0, 1.0, 0.0)
    series_row = term
    series_col = jnp.zeros((K, 1), F32)
    for degree in range(1, DEGREES):
        if degree % 2:
            term = jnp.sum((time_step * h) * term, axis=1, keepdims=True) * (1.0 / degree)
            series_col = series_col + term
        else:
            term = jnp.sum((time_step * ht) * term, axis=0, keepdims=True) * (1.0 / degree)
            series_row = series_row + term
    weights = [(pick(series_row, k) + series_col[k:k + 1, :]) * norm_zero for k in range(K)]

    def sum_chunk(i, c):
        rows = pl.ds(pl.multiple_of(i * ROWS, ROWS), ROWS)
        total = weights[0] * basis[0, rows, :]
        for k in range(1, K):
            total = total + weights[k] * basis[k, rows, :]
        evolved[rows, :] = total
        return c

    lax.fori_loop(0, width // ROWS, sum_chunk, 0)

    for t in range(nrow):
        @pl.when(r % rep == t % rep)
        def _():
            put(evolved.at[pl.ds(t * lr, lr), :], out.at[sector, :, my_cols], o_send.at[t],
                o_recv.at[sector, p], (base + owner, t), (r == t) & (p == owner))

    for s in range(S):
        for c in range(2):
            got(out.at[s, :, pl.ds(c * half, half)], o_recv.at[s, c])
    for t in range(nrow):
        @pl.when(r % rep == t % rep)
        def _():
            put_done(evolved.at[pl.ds(t * lr, lr), :], o_send.at[t], (r == t) & (p == owner))
    meta_copy.wait_send()
    for s, j, t in targets:
        for c in range(2):
            put_done(theta_piece(s, c), th_send.at[s, j, c], (t == r) & (p == c))

    def env_done(w, carry):
        for s, j, t in targets:
            for c in range(2):
                put_done(right.at[s, w, :, pl.ds(c * half, half)], r_send.at[w, s, j, c], (t == r) & (p == c))
            put_done(left.at[s, w], l_send.at[w, s, j], (t == r) & (p == w % 2))
        return carry

    lax.fori_loop(0, W, env_done, 0)

    def forward_done(pair, carry):
        forward_copy(2 * pair + p).wait_send()
        return carry

    lax.fori_loop(0, W // 2, forward_done, 0)


def local(ngrp, nrow, theta, left_env, right_env, lengths):
    S, lr, width = theta.shape
    W = left_env.shape[1]
    half = width // 2
    n = ngrp * nrow
    rep = nrow // (2 * S)
    K = KRYLOV
    dma = pltpu.SemaphoreType.DMA
    vmem = pl.BlockSpec(memory_space=pltpu.VMEM)
    hbm = pl.BlockSpec(memory_space=pl.ANY)
    return pl.pallas_call(
        functools.partial(kernel, ngrp, nrow),
        out_shape=(jax.ShapeDtypeStruct(theta.shape, F32), jax.ShapeDtypeStruct((K, K), F32)),
        in_specs=[pl.BlockSpec(memory_space=pltpu.SMEM), vmem, hbm, hbm],
        out_specs=(hbm, vmem),
        scratch_shapes=[
            pltpu.VMEM((S, lr, width), F32),
            pltpu.VMEM((2, 8 * ((2 * S + 7) // 8), 128), F32),
            pltpu.VMEM((W, width, width), BF16),
            pltpu.VMEM((width, W * width), BF16),
            pltpu.VMEM((W, width, half), BF16),
            pltpu.VMEM((W * width, half), BF16),
            pltpu.VMEM((K, width, half), F32),
            pltpu.VMEM((K, width, width), BF16),
            pltpu.VMEM((width, half), F32),
            pltpu.VMEM((width, half), F32),
            pltpu.VMEM((K + 1, 1, 128), F32),
            pltpu.VMEM((K + 1, n, 1, 128), F32),
            pltpu.VMEM((K, 128), F32),
            pltpu.VMEM((width, half), F32),
            dma((S, rep, 2)), dma((nrow,)), dma, dma,
            dma((W, S, rep)), dma((W, nrow)), dma((W,)), dma((W,)),
            dma((W, S, rep, 2)), dma((W, nrow)), dma((K,)), dma((K,)),
            dma((K + 1,)), dma((K + 1,)), dma((nrow,)), dma((S, 2)),
        ],
        compiler_params=pltpu.CompilerParams(collective_id=0, has_side_effects=True,
                                             vmem_limit_bytes=60 * 1024 * 1024),
    )(lengths, theta, left_env, right_env)


def solution(mesh):
    return jax.shard_map(
        functools.partial(local, mesh.shape["grp"], mesh.shape["row"]),
        mesh=mesh,
        in_specs=(
            P("grp", "row", None),
            P("grp", None, "row", None),
            P("grp", None, "row", None),
            P("grp", None),
        ),
        out_specs=(P("grp", "row", None), P()),
        check_vma=False,
    )
```

```python
import functools

import jax
import jax.numpy as jnp
from jax import lax
from jax.experimental import pallas as pl
from jax.experimental.pallas import tpu as pltpu
from jax.sharding import PartitionSpec as P

KRYLOV = 8
DEGREES = 19
ROWS = 32

epsilon = 1e-06
time_step = 0.5
MESH = pl.DeviceIdType.MESH
F32 = jnp.float32
BF16 = jnp.bfloat16


def kernel(ngrp, nrow, lengths, theta, left, right, out, hess,
           masked, meta, l_land, l_t, r_land, q, basis, img, v, acc, live, msg, slots, h_t, evolved, landed,
           th_send, th_recv, meta_send, meta_recv, l_send, l_recv, f_send, f_recv,
           r_send, r_recv, v_send, v_recv, m_send, m_recv, o_send, o_recv):
    S, lr, width = theta.shape
    W = left.shape[1]
    half = width // 2
    K = KRYLOV
    n = ngrp * nrow
    rep = nrow // (2 * S)
    g, r = lax.axis_index("grp"), lax.axis_index("row")
    me = g * nrow + r
    p = g % 2
    base = g - p
    partner = (base + 1 - p, r)
    owner = r // (S * rep)
    sector = (r // rep) % S
    my_cols = pl.ds(pl.multiple_of(p * half, half), half)
    my_rows = pl.ds(pl.multiple_of(r * lr, lr), lr)

    barrier = pltpu.get_barrier_semaphore()

    def greet(o, c):
        t = (me + o) % n
        pl.semaphore_signal(barrier, inc=1, device_id=(t // nrow, t % nrow), device_id_type=MESH)
        return c

    lax.fori_loop(1, n, greet, 0)

    lane = lax.broadcasted_iota(jnp.int32, (1, 128), 1)
    square = jnp.zeros((8, width), F32)
    for s in range(S):
        for k in range(2):
            meta[p, pl.ds(2 * s + k, 1), :] = jnp.full((1, 128), lengths[s, k].astype(F32))
        row_ids = r * lr + lax.broadcasted_iota(jnp.int32, (lr, width), 0)
        col_ids = lax.broadcasted_iota(jnp.int32, (lr, width), 1)
        keep = (row_ids < lengths[s, 0]) & (col_ids < lengths[s, 1])
        block = jnp.where(keep, theta[s], 0.0)
        masked[s] = block
        square = square + jnp.sum((block * block).reshape(lr // 8, 8, width), axis=0)
    for k in range(1, K):
        basis[k] = jnp.zeros((width, half), F32)
        img[k] = jnp.zeros((width, half), F32)
    h_t[...] = jnp.zeros_like(h_t)

    pl.semaphore_wait(barrier, n - 1)

    def put(src, dst, send, recv, dev, own):
        @pl.when(own)
        def _():
            pltpu.make_async_copy(src, dst, recv).start()

        @pl.when(jnp.logical_not(own))
        def _():
            pltpu.make_async_remote_copy(src_ref=src, dst_ref=dst, send_sem=send, recv_sem=recv,
                                         device_id=dev, device_id_type=MESH).start()

    def put_done(src, send, own):
        @pl.when(jnp.logical_not(own))
        def _():
            pltpu.make_async_copy(src, src, send).wait()

    def got(dst, recv):
        pltpu.make_async_copy(dst, dst, recv).wait()

    def share(k, row):
        msg[k] = row
        slots[k, me] = row

        def one(o, c):
            t = (me + o) % n
            pltpu.make_async_remote_copy(src_ref=msg.at[k], dst_ref=slots.at[k, me], send_sem=m_send.at[k],
                                         recv_sem=m_recv.at[k], device_id=(t // nrow, t % nrow),
                                         device_id_type=MESH).start()
            return c

        lax.fori_loop(1, n, one, 0)

    def shared(k):
        rest = slots.at[k, pl.ds(0, n - 1)]
        pltpu.make_async_copy(rest, rest, m_recv.at[k]).wait()
        pltpu.make_async_copy(rest, rest, m_send.at[k]).wait()
        return jnp.sum(slots[k], axis=0)

    def pick(row, i):
        return jnp.sum(jnp.where(lane == i, row, 0.0), axis=1, keepdims=True)

    meta_copy = pltpu.make_async_remote_copy(src_ref=meta.at[p], dst_ref=meta.at[p], send_sem=meta_send,
                                             recv_sem=meta_recv, device_id=partner, device_id_type=MESH)
    meta_copy.start()
    share(K, jnp.where(lane == 0, jnp.sum(square), 0.0))

    targets = [(s, j, (p * S + s) * rep + j) for s in range(S) for j in range(rep)]

    def theta_piece(s, c):
        return masked.at[s, :, pl.ds(c * half, half)]

    for s, j, t in targets:
        for c in range(2):
            put(theta_piece(s, c), basis.at[0, my_rows, :], th_send.at[s, j, c], th_recv.at[r],
                (base + c, t), (t == r) & (p == c))

    def send_left(w, carry):
        for s, j, t in targets:
            put(left.at[s, w], l_land.at[w, my_rows, :], l_send.at[w, s, j], l_recv.at[w, r],
                (base + w % 2, t), (t == r) & (p == w % 2))
        return carry

    def send_right(w, carry):
        for s, j, t in targets:
            for c in range(2):
                put(right.at[s, w, :, pl.ds(c * half, half)], r_land.at[w, my_rows, :],
                    r_send.at[w, s, j, c], r_recv.at[w, r], (base + c, t), (t == r) & (p == c))
        return carry

    lax.fori_loop(0, 2, send_left, 0)
    lax.fori_loop(0, W - 2, lambda w, c: send_right(w, send_left(w + 2, c)), 0)
    lax.fori_loop(W - 2, W, send_right, 0)

    pltpu.make_async_copy(meta.at[1 - p], meta.at[1 - p], meta_recv).wait()
    a_len = meta[owner, pl.ds(2 * sector, 1), :]
    c_len = meta[owner, pl.ds(2 * sector + 1, 1), :]
    a_len = jnp.concatenate([a_len] * (half // 128), axis=1)
    c_len = jnp.concatenate([c_len] * (half // 128), axis=1)
    row_ids = lax.broadcasted_iota(jnp.int32, (width, half), 0).astype(F32)
    col_ids = (p * half + lax.broadcasted_iota(jnp.int32, (width, half), 1)).astype(F32)
    live[...] = jnp.where((row_ids < a_len) & (col_ids < c_len), 1.0, 0.0)

    def v_copy(j):
        return pltpu.make_async_remote_copy(src_ref=v.at[j, :, my_cols], dst_ref=v.at[j, :, my_cols],
                                            send_sem=v_send.at[j], recv_sem=v_recv.at[j],
                                            device_id=partner, device_id_type=MESH)

    norm_zero = jnp.sqrt(pick(shared(K), 0) + epsilon)
    for i in range(nrow):
        got(basis.at[0, pl.ds(i * lr, lr), :], th_recv.at[i])

    def start_chunk(i, c):
        rows = pl.ds(pl.multiple_of(i * ROWS, ROWS), ROWS)
        b = basis[0, rows, :] / norm_zero
        basis[0, rows, :] = b
        v[0, rows, my_cols] = b.astype(BF16)
        return c

    lax.fori_loop(0, width // ROWS, start_chunk, 0)
    first = v_copy(0)
    first.start()
    first.wait()

    def forward_copy(w):
        return pltpu.make_async_remote_copy(src_ref=l_land.at[w], dst_ref=l_land.at[w], send_sem=f_send.at[w],
                                            recv_sem=f_recv.at[w], device_id=partner, device_id_type=MESH)

    acc[...] = jnp.zeros((width, half), F32)

    def turn(w):
        at = pl.ds(pl.multiple_of(w * width, width), width)
        l_t[:, at] = l_land[w].T

    def image_zero(pair, carry):
        mine, theirs = 2 * pair + p, 2 * pair + 1 - p
        for i in range(nrow):
            got(l_land.at[mine, pl.ds(i * lr, lr), :], l_recv.at[mine, i])
        forward_copy(mine).start()
        turn(mine)
        got(l_land.at[theirs], f_recv.at[theirs])
        turn(theirs)
        for step in range(2):
            w = 2 * pair + step
            for i in range(nrow):
                got(r_land.at[w, pl.ds(i * lr, lr), :], r_recv.at[w, i])
            at = pl.ds(pl.multiple_of(w * width, width), width)
            q[at, :] = jnp.dot(v[0], r_land[w], preferred_element_type=F32).astype(BF16)
        at = pl.ds(pl.multiple_of(pair * 2 * width, 2 * width), 2 * width)
        acc[...] += jnp.dot(l_t[:, at], q[at, :], preferred_element_type=F32)
        return carry

    lax.fori_loop(0, W // 2, image_zero, 0)

    counts = jnp.where(r % rep == 0, 1.0, 0.0)

    def sweep(j, update, shift):
        def chunk(i, sums):
            rows = pl.ds(pl.multiple_of(i * ROWS, ROWS), ROWS)
            b, u = update(rows)
            new = [sums[k] + jnp.sum((basis[k, rows, :] * u).reshape(ROWS // 8, 8, half), axis=0) for k in range(K)]
            new.append(sums[K] + jnp.sum((u * u).reshape(ROWS // 8, 8, half), axis=0))
            v[j + 1, rows, my_cols] = (u - shift * b).astype(BF16)
            return tuple(new)

        zero = jnp.zeros((8, half), F32)
        sums = lax.fori_loop(0, width // ROWS, chunk, (zero,) * (K + 1))

        @pl.when(j + 1 < K)
        def _():
            v_copy(j + 1).start()

        row = jnp.zeros((1, 128), F32)
        for k in range(K + 1):
            row = jnp.where(lane == k, jnp.sum(sums[k]), row)
        share(j, row * counts)

    def first_update(rows):
        u = acc[rows, :] * live[rows, :]
        img[0, rows, :] = u
        return basis[0, rows, :], u

    no_shift = jnp.zeros((1, 1), F32)
    sweep(0, first_update, no_shift)

    def step(j, shift):
        copy = v_copy(j + 1)
        copy.wait()
        vec = v.at[j + 1]
        for w in range(W):
            q[w * width:(w + 1) * width, :] = jnp.dot(vec[...], r_land[w], preferred_element_type=F32).astype(BF16)
        acc[...] = jnp.dot(l_t[...], q[...], preferred_element_type=F32)

        row = shared(j)
        dots = jnp.where(lane < K, row, 0.0)
        left_over = pick(row, K) - jnp.sum(dots * dots, axis=1, keepdims=True)
        beta = jnp.sqrt(jnp.maximum(left_over, 0.0) + epsilon)
        h_t[pl.ds(j, 1), :] = jnp.where(lane == j + 1, beta, dots)
        scale = 1.0 / beta
        rest = jnp.where(lane == j, dots - shift, dots)
        for_basis = [pick(dots, k) * scale for k in range(K)]
        for_image = [pick(rest, k) * scale for k in range(K)]

        def update(rows):
            b = img[j, rows, :] * scale
            u = acc[rows, :] * (live[rows, :] * scale)
            for k in range(K):
                b = b - for_basis[k] * basis[k, rows, :]
                u = u - for_image[k] * img[k, rows, :]
            basis[j + 1, rows, :] = b
            img[j + 1, rows, :] = u
            return b, u

        shift = pick(dots, j)
        sweep(j + 1, update, shift)
        return shift

    lax.fori_loop(0, K - 1, step, no_shift)
    row = shared(K - 1)
    h_t[pl.ds(K - 1, 1), :] = jnp.where(lane < K, row, 0.0)

    ht = h_t[...]
    sub = lax.broadcasted_iota(jnp.int32, (K, 128), 0)
    lanes = lax.broadcasted_iota(jnp.int32, (K, 128), 1)
    h = jnp.zeros((K, 128), F32)
    for j in range(K):
        column = jnp.sum(jnp.where(lanes == sub, ht[j:j + 1, :], 0.0), axis=1, keepdims=True)
        h = jnp.where(lanes == j, column, h)
    hess[...] = h[:, :K]
    term = jnp.where(lane == 0, 1.0, 0.0)
    series_row = term
    series_col = jnp.zeros((K, 1), F32)
    for degree in range(1, DEGREES):
        if degree % 2:
            term = jnp.sum((time_step * h) * term, axis=1, keepdims=True) * (1.0 / degree)
            series_col = series_col + term
        else:
            term = jnp.sum((time_step * ht) * term, axis=0, keepdims=True) * (1.0 / degree)
            series_row = series_row + term
    weights = [(pick(series_row, k) + series_col[k:k + 1, :]) * norm_zero for k in range(K)]

    def sum_chunk(i, c):
        rows = pl.ds(pl.multiple_of(i * ROWS, ROWS), ROWS)
        total = weights[0] * basis[0, rows, :]
        for k in range(1, K):
            total = total + weights[k] * basis[k, rows, :]
        evolved[rows, :] = total.astype(BF16)
        return c

    lax.fori_loop(0, width // ROWS, sum_chunk, 0)

    for t in range(nrow):
        @pl.when(r % rep == t % rep)
        def _():
            put(evolved.at[pl.ds(t * lr, lr), :], landed.at[sector, :, my_cols], o_send.at[t],
                o_recv.at[sector, p], (base + owner, t), (r == t) & (p == owner))

    for s in range(S):
        for c in range(2):
            got(landed.at[s, :, pl.ds(c * half, half)], o_recv.at[s, c])
        out[s] = landed[s].astype(F32)
    for t in range(nrow):
        @pl.when(r % rep == t % rep)
        def _():
            put_done(evolved.at[pl.ds(t * lr, lr), :], o_send.at[t], (r == t) & (p == owner))
    meta_copy.wait_send()
    for s, j, t in targets:
        for c in range(2):
            put_done(theta_piece(s, c), th_send.at[s, j, c], (t == r) & (p == c))

    def env_done(w, carry):
        for s, j, t in targets:
            for c in range(2):
                put_done(right.at[s, w, :, pl.ds(c * half, half)], r_send.at[w, s, j, c], (t == r) & (p == c))
            put_done(left.at[s, w], l_send.at[w, s, j], (t == r) & (p == w % 2))
        return carry

    lax.fori_loop(0, W, env_done, 0)

    def forward_done(pair, carry):
        forward_copy(2 * pair + p).wait_send()
        return carry

    lax.fori_loop(0, W // 2, forward_done, 0)


def local(ngrp, nrow, theta, left_env, right_env, lengths):
    S, lr, width = theta.shape
    W = left_env.shape[1]
    half = width // 2
    n = ngrp * nrow
    rep = nrow // (2 * S)
    K = KRYLOV
    dma = pltpu.SemaphoreType.DMA
    vmem = pl.BlockSpec(memory_space=pltpu.VMEM)
    hbm = pl.BlockSpec(memory_space=pl.ANY)
    return pl.pallas_call(
        functools.partial(kernel, ngrp, nrow),
        out_shape=(jax.ShapeDtypeStruct(theta.shape, F32), jax.ShapeDtypeStruct((K, K), F32)),
        in_specs=[pl.BlockSpec(memory_space=pltpu.SMEM), vmem, hbm, hbm],
        out_specs=(vmem, vmem),
        scratch_shapes=[
            pltpu.VMEM((S, lr, width), F32),
            pltpu.VMEM((2, 8 * ((2 * S + 7) // 8), 128), F32),
            pltpu.VMEM((W, width, width), BF16),
            pltpu.VMEM((width, W * width), BF16),
            pltpu.VMEM((W, width, half), BF16),
            pltpu.VMEM((W * width, half), BF16),
            pltpu.VMEM((K, width, half), F32),
            pltpu.VMEM((K, width, half), F32),
            pltpu.VMEM((K + 1, width, width), BF16),
            pltpu.VMEM((width, half), F32),
            pltpu.VMEM((width, half), F32),
            pltpu.VMEM((K + 1, 1, 128), F32),
            pltpu.VMEM((K + 1, n, 1, 128), F32),
            pltpu.VMEM((K, 128), F32),
            pltpu.VMEM((width, half), BF16),
            pltpu.VMEM((S, lr, width), BF16),
            dma((S, rep, 2)), dma((nrow,)), dma, dma,
            dma((W, S, rep)), dma((W, nrow)), dma((W,)), dma((W,)),
            dma((W, S, rep, 2)), dma((W, nrow)), dma((K,)), dma((K,)),
            dma((K + 1,)), dma((K + 1,)), dma((nrow,)), dma((S, 2)),
        ],
        compiler_params=pltpu.CompilerParams(collective_id=0, has_side_effects=True,
                                             vmem_limit_bytes=60 * 1024 * 1024),
    )(lengths, theta, left_env, right_env)


def solution(mesh):
    return jax.shard_map(
        functools.partial(local, mesh.shape["grp"], mesh.shape["row"]),
        mesh=mesh,
        in_specs=(
            P("grp", "row", None),
            P("grp", None, "row", None),
            P("grp", None, "row", None),
            P("grp", None),
        ),
        out_specs=(P("grp", "row", None), P()),
        check_vma=False,
    )
```

```python
import functools

import jax
import jax.numpy as jnp
from jax import lax
from jax.experimental import pallas as pl
from jax.experimental.pallas import tpu as pltpu
from jax.sharding import PartitionSpec as P

KRYLOV = 8
DEGREES = 19
ROWS = 32

epsilon = 1e-06
time_step = 0.5
MESH = pl.DeviceIdType.MESH
F32 = jnp.float32
BF16 = jnp.bfloat16


def kernel(ngrp, nrow, lengths, theta, left, right, out, hess,
           masked, packed, meta, l_land, l_t, r_land, q, basis, img, v, acc, live, msg, slots, h_t, evolved, landed,
           th_send, th_recv, meta_send, meta_recv, l_send, l_recv, f_send, f_recv,
           r_send, r_recv, v_send, v_recv, m_send, m_recv, o_send, o_recv):
    S, lr, width = theta.shape
    W = left.shape[1]
    half = width // 2
    K = KRYLOV
    n = ngrp * nrow
    rep = nrow // (2 * S)
    g, r = lax.axis_index("grp"), lax.axis_index("row")
    me = g * nrow + r
    p = g % 2
    base = g - p
    partner = (base + 1 - p, r)
    owner = r // (S * rep)
    sector = (r // rep) % S
    my_cols = pl.ds(pl.multiple_of(p * half, half), half)
    my_rows = pl.ds(pl.multiple_of(r * lr, lr), lr)

    barrier = pltpu.get_barrier_semaphore()

    def greet(o, c):
        t = (me + o) % n
        pl.semaphore_signal(barrier, inc=1, device_id=(t // nrow, t % nrow), device_id_type=MESH)
        return c

    lax.fori_loop(1, n, greet, 0)

    lane = lax.broadcasted_iota(jnp.int32, (1, 128), 1)
    square = jnp.zeros((8, width), F32)
    for s in range(S):
        for k in range(2):
            meta[p, pl.ds(2 * s + k, 1), :] = jnp.full((1, 128), lengths[s, k].astype(F32))
        row_ids = r * lr + lax.broadcasted_iota(jnp.int32, (lr, width), 0)
        col_ids = lax.broadcasted_iota(jnp.int32, (lr, width), 1)
        keep = (row_ids < lengths[s, 0]) & (col_ids < lengths[s, 1])
        block = jnp.where(keep, theta[s], 0.0)
        masked[s] = block
        square = square + jnp.sum((block * block).reshape(lr // 8, 8, width), axis=0)
    for k in range(1, K):
        basis[k] = jnp.zeros((width, half), F32)
        img[k] = jnp.zeros((width, half), F32)
    h_t[...] = jnp.zeros_like(h_t)

    pl.semaphore_wait(barrier, n - 1)

    def put(src, dst, send, recv, dev, own):
        @pl.when(own)
        def _():
            pltpu.make_async_copy(src, dst, recv).start()

        @pl.when(jnp.logical_not(own))
        def _():
            pltpu.make_async_remote_copy(src_ref=src, dst_ref=dst, send_sem=send, recv_sem=recv,
                                         device_id=dev, device_id_type=MESH).start()

    def put_done(src, send, own):
        @pl.when(jnp.logical_not(own))
        def _():
            pltpu.make_async_copy(src, src, send).wait()

    def got(dst, recv):
        pltpu.make_async_copy(dst, dst, recv).wait()

    def share(k, row):
        msg[k] = row
        slots[k, me] = row

        def one(o, c):
            t = (me + o) % n
            pltpu.make_async_remote_copy(src_ref=msg.at[k], dst_ref=slots.at[k, me], send_sem=m_send.at[k],
                                         recv_sem=m_recv.at[k], device_id=(t // nrow, t % nrow),
                                         device_id_type=MESH).start()
            return c

        lax.fori_loop(1, n, one, 0)

    def shared(k):
        rest = slots.at[k, pl.ds(0, n - 1)]
        pltpu.make_async_copy(rest, rest, m_recv.at[k]).wait()
        pltpu.make_async_copy(rest, rest, m_send.at[k]).wait()
        return jnp.sum(slots[k], axis=0)

    def pick(row, i):
        return jnp.sum(jnp.where(lane == i, row, 0.0), axis=1, keepdims=True)

    meta_copy = pltpu.make_async_remote_copy(src_ref=meta.at[p], dst_ref=meta.at[p], send_sem=meta_send,
                                             recv_sem=meta_recv, device_id=partner, device_id_type=MESH)
    meta_copy.start()
    share(K, jnp.where(lane == 0, jnp.sum(square), 0.0))

    targets = [(s, j, (p * S + s) * rep + j) for s in range(S) for j in range(rep)]

    def theta_piece(s, c):
        return packed.at[s, :, pl.ds(c * half, half)]

    def send_left(w, carry):
        for s, j, t in targets:
            put(left.at[s, w], l_land.at[w, my_rows, :], l_send.at[w, s, j], l_recv.at[w, r],
                (base + w % 2, t), (t == r) & (p == w % 2))
        return carry

    def send_right(w, carry):
        for s, j, t in targets:
            for c in range(2):
                put(right.at[s, w, :, pl.ds(c * half, half)], r_land.at[w, my_rows, :],
                    r_send.at[w, s, j, c], r_recv.at[w, r], (base + c, t), (t == r) & (p == c))
        return carry

    lax.fori_loop(0, 2, send_left, 0)
    pltpu.make_async_copy(meta.at[1 - p], meta.at[1 - p], meta_recv).wait()
    a_len = meta[owner, pl.ds(2 * sector, 1), :]
    c_len = meta[owner, pl.ds(2 * sector + 1, 1), :]
    a_len = jnp.concatenate([a_len] * (half // 128), axis=1)
    c_len = jnp.concatenate([c_len] * (half // 128), axis=1)
    row_ids = lax.broadcasted_iota(jnp.int32, (width, half), 0).astype(F32)
    col_ids = (p * half + lax.broadcasted_iota(jnp.int32, (width, half), 1)).astype(F32)
    live[...] = jnp.where((row_ids < a_len) & (col_ids < c_len), 1.0, 0.0)

    norm_zero = jnp.sqrt(pick(shared(K), 0) + epsilon)
    for s in range(S):
        packed[s] = (masked[s] / norm_zero).astype(BF16)
    for s, j, t in targets:
        for c in range(2):
            put(theta_piece(s, c), v.at[0, my_rows, pl.ds(c * half, half)], th_send.at[s, j, c], th_recv.at[r],
                (base + c, t), (t == r) & (p == c))
    lax.fori_loop(0, W - 2, lambda w, c: send_right(w, send_left(w + 2, c)), 0)
    lax.fori_loop(W - 2, W, send_right, 0)

    def v_copy(j):
        return pltpu.make_async_remote_copy(src_ref=v.at[j, :, my_cols], dst_ref=v.at[j, :, my_cols],
                                            send_sem=v_send.at[j], recv_sem=v_recv.at[j],
                                            device_id=partner, device_id_type=MESH)

    for i in range(nrow):
        got(v.at[0, pl.ds(i * lr, lr), my_cols], th_recv.at[i])
    first = v_copy(0)
    first.start()
    def start_chunk(i, c):
        rows = pl.ds(pl.multiple_of(i * ROWS, ROWS), ROWS)
        basis[0, rows, :] = v[0, rows, my_cols].astype(F32)
        return c

    lax.fori_loop(0, width // ROWS, start_chunk, 0)
    first.wait()

    def forward_copy(w):
        return pltpu.make_async_remote_copy(src_ref=l_land.at[w], dst_ref=l_land.at[w], send_sem=f_send.at[w],
                                            recv_sem=f_recv.at[w], device_id=partner, device_id_type=MESH)

    acc[...] = jnp.zeros((width, half), F32)

    def turn(w):
        at = pl.ds(pl.multiple_of(w * width, width), width)
        l_t[:, at] = l_land[w].T

    def image_zero(pair, carry):
        mine, theirs = 2 * pair + p, 2 * pair + 1 - p
        for i in range(nrow):
            got(l_land.at[mine, pl.ds(i * lr, lr), :], l_recv.at[mine, i])
        forward_copy(mine).start()
        turn(mine)
        got(l_land.at[theirs], f_recv.at[theirs])
        turn(theirs)
        for step in range(2):
            w = 2 * pair + step
            for i in range(nrow):
                got(r_land.at[w, pl.ds(i * lr, lr), :], r_recv.at[w, i])
            at = pl.ds(pl.multiple_of(w * width, width), width)
            q[at, :] = jnp.dot(v[0], r_land[w], preferred_element_type=F32).astype(BF16)
        at = pl.ds(pl.multiple_of(pair * 2 * width, 2 * width), 2 * width)
        acc[...] += jnp.dot(l_t[:, at], q[at, :], preferred_element_type=F32)
        return carry

    lax.fori_loop(0, W // 2, image_zero, 0)

    counts = jnp.where(r % rep == 0, 1.0, 0.0)

    def sweep(j, have, update, shift):
        def chunk(i, sums):
            rows = pl.ds(pl.multiple_of(i * ROWS, ROWS), ROWS)
            b, u = update(rows)
            new = [sums[k] + jnp.sum((basis[k, rows, :] * u).reshape(ROWS // 8, 8, half), axis=0)
                   for k in range(have)]
            new.append(sums[have] + jnp.sum((u * u).reshape(ROWS // 8, 8, half), axis=0))
            v[j + 1, rows, my_cols] = (u - shift * b).astype(BF16)
            return tuple(new)

        zero = jnp.zeros((8, half), F32)
        sums = lax.fori_loop(0, width // ROWS, chunk, (zero,) * (have + 1))

        @pl.when(j + 1 < K)
        def _():
            v_copy(j + 1).start()

        row = jnp.zeros((1, 128), F32)
        for k in range(have + 1):
            row = jnp.where(lane == (k if k < have else K), jnp.sum(sums[k]), row)
        share(j, row * counts)

    def first_update(rows):
        u = acc[rows, :] * live[rows, :]
        img[0, rows, :] = u
        return basis[0, rows, :], u

    no_shift = jnp.zeros((1, 1), F32)
    sweep(0, 1, first_update, no_shift)

    def step(have, j, carry):
        shift, trace = carry
        copy = v_copy(j + 1)
        copy.wait()
        vec = v.at[j + 1]
        for w in range(W):
            q[w * width:(w + 1) * width, :] = jnp.dot(vec[...], r_land[w], preferred_element_type=F32).astype(BF16)
        acc[...] = jnp.dot(l_t[...], q[...], preferred_element_type=F32)

        row = shared(j)
        dots = jnp.where(lane < K, row, 0.0)
        left_over = pick(row, K) - jnp.sum(dots * dots, axis=1, keepdims=True)
        beta = jnp.sqrt(jnp.maximum(left_over, 0.0) + epsilon)
        h_t[pl.ds(j, 1), :] = jnp.where(lane == j + 1, beta, dots)
        scale = 1.0 / beta
        rest = jnp.where(lane == j, dots - shift, dots)
        for_basis = [pick(dots, k) * scale for k in range(have - 1)]
        for_image = [pick(rest, k) * scale for k in range(have - 1)]
        trace = jnp.where(lane == j + 1, -scale * jnp.sum(dots * trace, axis=1, keepdims=True), trace)

        def update(rows):
            b = img[j, rows, :] * scale
            u = acc[rows, :] * (live[rows, :] * scale)
            for k in range(have - 1):
                b = b - for_basis[k] * basis[k, rows, :]
                u = u - for_image[k] * img[k, rows, :]
            basis[j + 1, rows, :] = b
            img[j + 1, rows, :] = u
            return b, u

        shift = pick(dots, j)
        sweep(j + 1, have, update, shift)
        return shift, trace

    carry = (no_shift, jnp.where(lane == 0, 1.0, 0.0))
    for start in range(0, K - 1, 2):
        end = min(start + 2, K - 1)
        carry = lax.fori_loop(start, end, functools.partial(step, end + 1), carry)
    trace = carry[1]
    row = shared(K - 1)
    h_t[pl.ds(K - 1, 1), :] = jnp.where(lane < K, row, 0.0)

    ht = h_t[...]
    sub = lax.broadcasted_iota(jnp.int32, (K, 128), 0)
    lanes = lax.broadcasted_iota(jnp.int32, (K, 128), 1)
    h = jnp.zeros((K, 128), F32)
    for j in range(K):
        column = jnp.sum(jnp.where(lanes == sub, ht[j:j + 1, :], 0.0), axis=1, keepdims=True)
        h = jnp.where(lanes == j, column, h)
    hess[...] = h[:, :K]
    term = jnp.where(lane == 0, 1.0, 0.0)
    series_row = term
    series_col = jnp.zeros((K, 1), F32)
    for degree in range(1, DEGREES):
        if degree % 2:
            term = jnp.sum((time_step * h) * term, axis=1, keepdims=True) * (1.0 / degree)
            series_col = series_col + term
        else:
            term = jnp.sum((time_step * ht) * term, axis=0, keepdims=True) * (1.0 / degree)
            series_row = series_row + term
    weights = [pick(series_row, k) + series_col[k:k + 1, :] for k in range(K)]
    fix = sum(pick(trace, k) * weights[k] for k in range(1, K))
    weights = weights[:1] + [weight * norm_zero for weight in weights[1:]]

    def sum_chunk(i, c):
        rows = pl.ds(pl.multiple_of(i * ROWS, ROWS), ROWS)
        total = weights[1] * basis[1, rows, :]
        for k in range(2, K):
            total = total + weights[k] * basis[k, rows, :]
        evolved[rows, :] = total.astype(BF16)
        return c

    lax.fori_loop(0, width // ROWS, sum_chunk, 0)

    for t in range(nrow):
        @pl.when(r % rep == t % rep)
        def _():
            put(evolved.at[pl.ds(t * lr, lr), :], landed.at[sector, :, my_cols], o_send.at[t],
                o_recv.at[sector, p], (base + owner, t), (r == t) & (p == owner))

    for s in range(S):
        for c in range(2):
            got(landed.at[s, :, pl.ds(c * half, half)], o_recv.at[s, c])
        out[s] = landed[s].astype(F32) + weights[0] * masked[s]
        out[s] += fix * (masked[s] - norm_zero * packed[s].astype(F32))
    for t in range(nrow):
        @pl.when(r % rep == t % rep)
        def _():
            put_done(evolved.at[pl.ds(t * lr, lr), :], o_send.at[t], (r == t) & (p == owner))
    meta_copy.wait_send()
    for s, j, t in targets:
        for c in range(2):
            put_done(theta_piece(s, c), th_send.at[s, j, c], (t == r) & (p == c))

    def env_done(w, carry):
        for s, j, t in targets:
            for c in range(2):
                put_done(right.at[s, w, :, pl.ds(c * half, half)], r_send.at[w, s, j, c], (t == r) & (p == c))
            put_done(left.at[s, w], l_send.at[w, s, j], (t == r) & (p == w % 2))
        return carry

    lax.fori_loop(0, W, env_done, 0)

    def forward_done(pair, carry):
        forward_copy(2 * pair + p).wait_send()
        return carry

    lax.fori_loop(0, W // 2, forward_done, 0)


def local(ngrp, nrow, theta, left_env, right_env, lengths):
    S, lr, width = theta.shape
    W = left_env.shape[1]
    half = width // 2
    n = ngrp * nrow
    rep = nrow // (2 * S)
    K = KRYLOV
    dma = pltpu.SemaphoreType.DMA
    vmem = pl.BlockSpec(memory_space=pltpu.VMEM)
    hbm = pl.BlockSpec(memory_space=pl.ANY)
    return pl.pallas_call(
        functools.partial(kernel, ngrp, nrow),
        out_shape=(jax.ShapeDtypeStruct(theta.shape, F32), jax.ShapeDtypeStruct((K, K), F32)),
        in_specs=[pl.BlockSpec(memory_space=pltpu.SMEM), vmem, hbm, hbm],
        out_specs=(vmem, vmem),
        scratch_shapes=[
            pltpu.VMEM((S, lr, width), F32),
            pltpu.VMEM((S, lr, width), BF16),
            pltpu.VMEM((2, 8 * ((2 * S + 7) // 8), 128), F32),
            pltpu.VMEM((W, width, width), BF16),
            pltpu.VMEM((width, W * width), BF16),
            pltpu.VMEM((W, width, half), BF16),
            pltpu.VMEM((W * width, half), BF16),
            pltpu.VMEM((K, width, half), F32),
            pltpu.VMEM((K, width, half), F32),
            pltpu.VMEM((K + 1, width, width), BF16),
            pltpu.VMEM((width, half), F32),
            pltpu.VMEM((width, half), F32),
            pltpu.VMEM((K + 1, 1, 128), F32),
            pltpu.VMEM((K + 1, n, 1, 128), F32),
            pltpu.VMEM((K, 128), F32),
            pltpu.VMEM((width, half), BF16),
            pltpu.VMEM((S, lr, width), BF16),
            dma((S, rep, 2)), dma((nrow,)), dma, dma,
            dma((W, S, rep)), dma((W, nrow)), dma((W,)), dma((W,)),
            dma((W, S, rep, 2)), dma((W, nrow)), dma((K,)), dma((K,)),
            dma((K + 1,)), dma((K + 1,)), dma((nrow,)), dma((S, 2)),
        ],
        compiler_params=pltpu.CompilerParams(collective_id=0, has_side_effects=True,
                                             vmem_limit_bytes=60 * 1024 * 1024),
    )(lengths, theta, left_env, right_env)


def solution(mesh):
    return jax.shard_map(
        functools.partial(local, mesh.shape["grp"], mesh.shape["row"]),
        mesh=mesh,
        in_specs=(
            P("grp", "row", None),
            P("grp", None, "row", None),
            P("grp", None, "row", None),
            P("grp", None),
        ),
        out_specs=(P("grp", "row", None), P()),
        check_vma=False,
    )
```

```python
import functools

import jax
import jax.numpy as jnp
from jax import lax
from jax.experimental import pallas as pl
from jax.experimental.pallas import tpu as pltpu
from jax.sharding import PartitionSpec as P

KRYLOV = 8
DEGREES = 19
ROWS = 32

epsilon = 1e-06
time_step = 0.5
MESH = pl.DeviceIdType.MESH
F32 = jnp.float32
BF16 = jnp.bfloat16


def kernel(ngrp, nrow, lengths, theta, left, right, landed, small,
           masked, packed, meta, l_land, l_t, r_land, q, basis, img, v, acc, live, msg, slots, h_t, evolved,
           th_send, th_recv, meta_send, meta_recv, l_send, l_recv, f_send, f_recv,
           r_send, r_recv, v_send, v_recv, m_send, m_recv, o_send, o_recv):
    S, lr, width = theta.shape
    W = left.shape[1]
    half = width // 2
    K = KRYLOV
    n = ngrp * nrow
    rep = nrow // (2 * S)
    g, r = lax.axis_index("grp"), lax.axis_index("row")
    me = g * nrow + r
    p = g % 2
    base = g - p
    partner = (base + 1 - p, r)
    owner = r // (S * rep)
    sector = (r // rep) % S
    my_cols = pl.ds(pl.multiple_of(p * half, half), half)
    my_rows = pl.ds(pl.multiple_of(r * lr, lr), lr)

    barrier = pltpu.get_barrier_semaphore()

    def greet(o, c):
        t = (me + o) % n
        pl.semaphore_signal(barrier, inc=1, device_id=(t // nrow, t % nrow), device_id_type=MESH)
        return c

    lax.fori_loop(1, n, greet, 0)

    lane = lax.broadcasted_iota(jnp.int32, (1, 128), 1)
    square = jnp.zeros((8, width), F32)
    for s in range(S):
        for k in range(2):
            meta[p, pl.ds(2 * s + k, 1), :] = jnp.full((1, 128), lengths[s, k].astype(F32))
        row_ids = r * lr + lax.broadcasted_iota(jnp.int32, (lr, width), 0)
        col_ids = lax.broadcasted_iota(jnp.int32, (lr, width), 1)
        keep = (row_ids < lengths[s, 0]) & (col_ids < lengths[s, 1])
        block = jnp.where(keep, theta[s], 0.0)
        masked[s] = block
        square = square + jnp.sum((block * block).reshape(lr // 8, 8, width), axis=0)
    for k in range(1, K):
        basis[k] = jnp.zeros((width, half), F32)
        img[k] = jnp.zeros((width, half), F32)
    h_t[...] = jnp.zeros_like(h_t)

    pl.semaphore_wait(barrier, n - 1)

    def put(src, dst, send, recv, dev, own):
        @pl.when(own)
        def _():
            pltpu.make_async_copy(src, dst, recv).start()

        @pl.when(jnp.logical_not(own))
        def _():
            pltpu.make_async_remote_copy(src_ref=src, dst_ref=dst, send_sem=send, recv_sem=recv,
                                         device_id=dev, device_id_type=MESH).start()

    def put_done(src, send, own):
        @pl.when(jnp.logical_not(own))
        def _():
            pltpu.make_async_copy(src, src, send).wait()

    def got(dst, recv):
        pltpu.make_async_copy(dst, dst, recv).wait()

    def share(k, row):
        msg[k] = row
        slots[k, me] = row

        def send(tg, tr):
            pltpu.make_async_remote_copy(src_ref=msg.at[k], dst_ref=slots.at[k, me], send_sem=m_send.at[k],
                                         recv_sem=m_recv.at[k], device_id=(tg, tr), device_id_type=MESH).start()

        def group(o, c):
            tg = (g + ngrp // 2 + o) % ngrp
            for d in range(nrow):
                send(tg, (r + d) % nrow)
            return c

        lax.fori_loop(0, ngrp - ngrp // 2, group, 0)
        lax.fori_loop(ngrp - ngrp // 2 + 1, ngrp, group, 0)
        for d in range(1, nrow):
            send(g, (r + d) % nrow)

    def shared(k):
        rest = slots.at[k, pl.ds(0, n - 1)]
        pltpu.make_async_copy(rest, rest, m_recv.at[k]).wait()
        pltpu.make_async_copy(rest, rest, m_send.at[k]).wait()
        return jnp.sum(slots[k], axis=0)

    def pick(row, i):
        return jnp.sum(jnp.where(lane == i, row, 0.0), axis=1, keepdims=True)

    meta_copy = pltpu.make_async_remote_copy(src_ref=meta.at[p], dst_ref=meta.at[p], send_sem=meta_send,
                                             recv_sem=meta_recv, device_id=partner, device_id_type=MESH)
    meta_copy.start()
    share(K, jnp.where(lane == 0, jnp.sum(square), 0.0))

    targets = [(s, j, (p * S + s) * rep + j) for s in range(S) for j in range(rep)]

    def theta_piece(s, c):
        return packed.at[s, :, pl.ds(c * half, half)]

    def send_left(w, carry):
        for s, j, t in targets:
            put(left.at[s, w], l_land.at[w, my_rows, :], l_send.at[w, s, j], l_recv.at[w, r],
                (base + w % 2, t), (t == r) & (p == w % 2))
        return carry

    def send_right(w, carry):
        for s, j, t in targets:
            for c in range(2):
                put(right.at[s, w, :, pl.ds(c * half, half)], r_land.at[w, my_rows, :],
                    r_send.at[w, s, j, c], r_recv.at[w, r], (base + c, t), (t == r) & (p == c))
        return carry

    lax.fori_loop(0, 2, send_left, 0)
    pltpu.make_async_copy(meta.at[1 - p], meta.at[1 - p], meta_recv).wait()
    a_len = meta[owner, pl.ds(2 * sector, 1), :]
    c_len = meta[owner, pl.ds(2 * sector + 1, 1), :]
    a_len = jnp.concatenate([a_len] * (half // 128), axis=1)
    c_len = jnp.concatenate([c_len] * (half // 128), axis=1)
    row_ids = lax.broadcasted_iota(jnp.int32, (width, half), 0).astype(F32)
    col_ids = (p * half + lax.broadcasted_iota(jnp.int32, (width, half), 1)).astype(F32)
    live[...] = jnp.where((row_ids < a_len) & (col_ids < c_len), 1.0, 0.0)

    norm_zero = jnp.sqrt(pick(shared(K), 0) + epsilon)
    for s in range(S):
        packed[s] = (masked[s] / norm_zero).astype(BF16)
    for s, j, t in targets:
        for c in range(2):
            put(theta_piece(s, c), v.at[0, my_rows, pl.ds(c * half, half)], th_send.at[s, j, c], th_recv.at[r],
                (base + c, t), (t == r) & (p == c))
    lax.fori_loop(0, W - 2, lambda w, c: send_right(w, send_left(w + 2, c)), 0)
    lax.fori_loop(W - 2, W, send_right, 0)

    def v_copy(j):
        return pltpu.make_async_remote_copy(src_ref=v.at[j, :, my_cols], dst_ref=v.at[j, :, my_cols],
                                            send_sem=v_send.at[j], recv_sem=v_recv.at[j],
                                            device_id=partner, device_id_type=MESH)

    for i in range(nrow):
        got(v.at[0, pl.ds(i * lr, lr), my_cols], th_recv.at[i])
    first = v_copy(0)
    first.start()
    def start_chunk(i, c):
        rows = pl.ds(pl.multiple_of(i * ROWS, ROWS), ROWS)
        basis[0, rows, :] = v[0, rows, my_cols].astype(F32)
        return c

    lax.fori_loop(0, width // ROWS, start_chunk, 0)
    first.wait()

    def forward_copy(w):
        return pltpu.make_async_remote_copy(src_ref=l_land.at[w], dst_ref=l_land.at[w], send_sem=f_send.at[w],
                                            recv_sem=f_recv.at[w], device_id=partner, device_id_type=MESH)

    acc[...] = jnp.zeros((width, half), F32)

    def turn(w):
        at = pl.ds(pl.multiple_of(w * width, width), width)
        l_t[:, at] = l_land[w].T

    def image_zero(pair, carry):
        mine, theirs = 2 * pair + p, 2 * pair + 1 - p
        for i in range(nrow):
            got(l_land.at[mine, pl.ds(i * lr, lr), :], l_recv.at[mine, i])
        forward_copy(mine).start()
        turn(mine)
        got(l_land.at[theirs], f_recv.at[theirs])
        turn(theirs)
        for step in range(2):
            w = 2 * pair + step
            for i in range(nrow):
                got(r_land.at[w, pl.ds(i * lr, lr), :], r_recv.at[w, i])
            at = pl.ds(pl.multiple_of(w * width, width), width)
            q[at, :] = jnp.dot(v[0], r_land[w], preferred_element_type=F32).astype(BF16)
        at = pl.ds(pl.multiple_of(pair * 2 * width, 2 * width), 2 * width)
        acc[...] += jnp.dot(l_t[:, at], q[at, :], preferred_element_type=F32)
        return carry

    lax.fori_loop(0, W // 2, image_zero, 0)

    counts = jnp.where(r % rep == 0, 1.0, 0.0)

    def sweep(j, have, update, shift):
        def chunk(i, sums):
            rows = pl.ds(pl.multiple_of(i * ROWS, ROWS), ROWS)
            b, u = update(rows)
            new = [sums[k] + jnp.sum((basis[k, rows, :] * u).reshape(ROWS // 8, 8, half), axis=0)
                   for k in range(have)]
            new.append(sums[have] + jnp.sum((u * u).reshape(ROWS // 8, 8, half), axis=0))
            v[j + 1, rows, my_cols] = (u - shift * b).astype(BF16)
            return tuple(new)

        zero = jnp.zeros((8, half), F32)
        sums = lax.fori_loop(0, width // ROWS, chunk, (zero,) * (have + 1))

        @pl.when(j + 1 < K)
        def _():
            v_copy(j + 1).start()

        row = jnp.zeros((1, 128), F32)
        for k in range(have + 1):
            row = jnp.where(lane == (k if k < have else K), jnp.sum(sums[k]), row)
        share(j, row * counts)

    def first_update(rows):
        u = acc[rows, :] * live[rows, :]
        img[0, rows, :] = u
        return basis[0, rows, :], u

    no_shift = jnp.zeros((1, 1), F32)
    sweep(0, 1, first_update, no_shift)

    def step(have, j, carry):
        shift, trace = carry
        copy = v_copy(j + 1)
        copy.wait()
        vec = v.at[j + 1]
        for w in range(W):
            q[w * width:(w + 1) * width, :] = jnp.dot(vec[...], r_land[w], preferred_element_type=F32).astype(BF16)
        acc[...] = jnp.dot(l_t[...], q[...], preferred_element_type=F32)

        row = shared(j)
        dots = jnp.where(lane < K, row, 0.0)
        left_over = pick(row, K) - jnp.sum(dots * dots, axis=1, keepdims=True)
        beta = jnp.sqrt(jnp.maximum(left_over, 0.0) + epsilon)
        h_t[pl.ds(j, 1), :] = jnp.where(lane == j + 1, beta, dots)
        scale = 1.0 / beta
        rest = jnp.where(lane == j, dots - shift, dots)
        for_basis = [pick(dots, k) * scale for k in range(have - 1)]
        for_image = [pick(rest, k) * scale for k in range(have - 1)]
        trace = jnp.where(lane == j + 1, -scale * jnp.sum(dots * trace, axis=1, keepdims=True), trace)

        def update(rows):
            b = img[j, rows, :] * scale
            u = acc[rows, :] * (live[rows, :] * scale)
            for k in range(have - 1):
                b = b - for_basis[k] * basis[k, rows, :]
                u = u - for_image[k] * img[k, rows, :]
            basis[j + 1, rows, :] = b
            img[j + 1, rows, :] = u
            return b, u

        shift = pick(dots, j)
        sweep(j + 1, have, update, shift)
        return shift, trace

    carry = (no_shift, jnp.where(lane == 0, 1.0, 0.0))
    for start in range(0, K - 1, 2):
        end = min(start + 2, K - 1)
        carry = lax.fori_loop(start, end, functools.partial(step, end + 1), carry)
    trace = carry[1]
    row = shared(K - 1)
    h_t[pl.ds(K - 1, 1), :] = jnp.where(lane < K, row, 0.0)

    ht = h_t[...]
    sub = lax.broadcasted_iota(jnp.int32, (K, 128), 0)
    lanes = lax.broadcasted_iota(jnp.int32, (K, 128), 1)
    h = jnp.zeros((K, 128), F32)
    for j in range(K):
        column = jnp.sum(jnp.where(lanes == sub, ht[j:j + 1, :], 0.0), axis=1, keepdims=True)
        h = jnp.where(lanes == j, column, h)
    term = jnp.where(lane == 0, 1.0, 0.0)
    series_row = term
    series_col = jnp.zeros((K, 1), F32)
    for degree in range(1, DEGREES):
        if degree % 2:
            term = jnp.sum((time_step * h) * term, axis=1, keepdims=True) * (1.0 / degree)
            series_col = series_col + term
        else:
            term = jnp.sum((time_step * ht) * term, axis=0, keepdims=True) * (1.0 / degree)
            series_row = series_row + term
    weights = [pick(series_row, k) + series_col[k:k + 1, :] for k in range(K)]
    fix = sum(pick(trace, k) * weights[k] for k in range(1, K))
    small[0:K, :] = h
    small[K:K + 1, :] = jnp.where(lane == 0, weights[0], jnp.where(lane == 1, fix, norm_zero))
    weights = weights[:1] + [weight * norm_zero for weight in weights[1:]]

    def sum_chunk(i, c):
        rows = pl.ds(pl.multiple_of(i * ROWS, ROWS), ROWS)
        total = weights[1] * basis[1, rows, :]
        for k in range(2, K):
            total = total + weights[k] * basis[k, rows, :]
        evolved[rows, :] = total.astype(BF16)
        return c

    lax.fori_loop(0, width // ROWS, sum_chunk, 0)

    for t in range(nrow):
        @pl.when(r % rep == t % rep)
        def _():
            put(evolved.at[pl.ds(t * lr, lr), :], landed.at[sector, :, my_cols], o_send.at[t],
                o_recv.at[sector, p], (base + owner, t), (r == t) & (p == owner))

    for s in range(S):
        for c in range(2):
            got(landed.at[s, :, pl.ds(c * half, half)], o_recv.at[s, c])
    for t in range(nrow):
        @pl.when(r % rep == t % rep)
        def _():
            put_done(evolved.at[pl.ds(t * lr, lr), :], o_send.at[t], (r == t) & (p == owner))
    meta_copy.wait_send()
    for s, j, t in targets:
        for c in range(2):
            put_done(theta_piece(s, c), th_send.at[s, j, c], (t == r) & (p == c))

    def env_done(w, carry):
        for s, j, t in targets:
            for c in range(2):
                put_done(right.at[s, w, :, pl.ds(c * half, half)], r_send.at[w, s, j, c], (t == r) & (p == c))
            put_done(left.at[s, w], l_send.at[w, s, j], (t == r) & (p == w % 2))
        return carry

    lax.fori_loop(0, W, env_done, 0)

    def forward_done(pair, carry):
        forward_copy(2 * pair + p).wait_send()
        return carry

    lax.fori_loop(0, W // 2, forward_done, 0)


def combine(lengths, theta, landed, small, out, hess):
    S, lr, width = theta.shape
    K = KRYLOV
    weight, fix, norm_zero = small[K:K + 1, 0:1], small[K:K + 1, 1:2], small[K:K + 1, 2:3]
    row_ids = lax.axis_index("row") * lr + lax.broadcasted_iota(jnp.int32, (lr, width), 0)
    col_ids = lax.broadcasted_iota(jnp.int32, (lr, width), 1)
    for s in range(S):
        masked = jnp.where((row_ids < lengths[s, 0]) & (col_ids < lengths[s, 1]), theta[s], 0.0)
        rounded = (masked / norm_zero).astype(BF16).astype(F32)
        out[s] = landed[s].astype(F32) + weight * masked + fix * (masked - norm_zero * rounded)
    hess[...] = small[:K, :K]


def local(ngrp, nrow, theta, left_env, right_env, lengths):
    S, lr, width = theta.shape
    W = left_env.shape[1]
    half = width // 2
    n = ngrp * nrow
    rep = nrow // (2 * S)
    K = KRYLOV
    dma = pltpu.SemaphoreType.DMA
    vmem = pl.BlockSpec(memory_space=pltpu.VMEM)
    hbm = pl.BlockSpec(memory_space=pl.ANY)
    landed, small = pl.pallas_call(
        functools.partial(kernel, ngrp, nrow),
        out_shape=(jax.ShapeDtypeStruct(theta.shape, BF16), jax.ShapeDtypeStruct((K + 8, 128), F32)),
        in_specs=[pl.BlockSpec(memory_space=pltpu.SMEM), vmem, hbm, hbm],
        out_specs=(hbm, vmem),
        scratch_shapes=[
            pltpu.VMEM((S, lr, width), F32),
            pltpu.VMEM((S, lr, width), BF16),
            pltpu.VMEM((2, 8 * ((2 * S + 7) // 8), 128), F32),
            pltpu.VMEM((W, width, width), BF16),
            pltpu.VMEM((width, W * width), BF16),
            pltpu.VMEM((W, width, half), BF16),
            pltpu.VMEM((W * width, half), BF16),
            pltpu.VMEM((K, width, half), F32),
            pltpu.VMEM((K, width, half), F32),
            pltpu.VMEM((K + 1, width, width), BF16),
            pltpu.VMEM((width, half), F32),
            pltpu.VMEM((width, half), F32),
            pltpu.VMEM((K + 1, 1, 128), F32),
            pltpu.VMEM((K + 1, n, 1, 128), F32),
            pltpu.VMEM((K, 128), F32),
            pltpu.VMEM((width, half), BF16),
            dma((S, rep, 2)), dma((nrow,)), dma, dma,
            dma((W, S, rep)), dma((W, nrow)), dma((W,)), dma((W,)),
            dma((W, S, rep, 2)), dma((W, nrow)), dma((K,)), dma((K,)),
            dma((K + 1,)), dma((K + 1,)), dma((nrow,)), dma((S, 2)),
        ],
        compiler_params=pltpu.CompilerParams(collective_id=0, has_side_effects=True,
                                             vmem_limit_bytes=60 * 1024 * 1024),
    )(lengths, theta, left_env, right_env)
    return pl.pallas_call(
        combine,
        out_shape=(jax.ShapeDtypeStruct(theta.shape, F32), jax.ShapeDtypeStruct((K, K), F32)),
        in_specs=[pl.BlockSpec(memory_space=pltpu.SMEM), vmem, vmem, vmem],
        out_specs=(vmem, vmem),
    )(lengths, theta, landed, small)


def solution(mesh):
    return jax.shard_map(
        functools.partial(local, mesh.shape["grp"], mesh.shape["row"]),
        mesh=mesh,
        in_specs=(
            P("grp", "row", None),
            P("grp", None, "row", None),
            P("grp", None, "row", None),
            P("grp", None),
        ),
        out_specs=(P("grp", "row", None), P()),
        check_vma=False,
    )
```
